32 devices in a mesh: dev: 32 (over z, y, x, core).
Axes of the slice: x: 2, y: 2, z: 4, core: 2. Of those that a mesh axis runs over, the one named last changes fastest.
Arguments:
- ensemble: float32 [128, 4, 256, 256], P('dev'), may hold values from -6 to 6
- flow_speed: float32 [2, 256, 256], replicated, may hold values from -0.6 to 0.6
- spreading_coefficient: float32 [4, 256, 256], replicated, may hold values from 0.01 to 0.12
- obs_values: float32 [2, 4096], replicated, may hold values from -6 to 6
- obs_var: float32 [4096], replicated, may hold values from 0.02 to 0.5
- obs_block: int32 [4096], replicated, may hold values from 0 to 16383, as said below
- readers: int32 [128, 128], replicated, may hold values from 0 to 4095, as said below
- counts: int32 [128], replicated, may hold values from 32 to 128
Outputs:
- analysed: float32 [128, 4, 256, 256], P('dev')
The draws below stay inside these ranges and needn't reach their ends.
Inputs may be any that keep to these rules, and one draw needn't show every extreme that they name: `obs_block`: observations are ordered by block row: observation i lies in block row (i * 64) // 4096. `readers`: each row lists distinct observations, mostly within three block rows of the patch; slots at or past the patch's count hold valid indices and are not read.
All inputs are finite; a program needn't handle non-finite values.
Results may differ from the reference program's by a relative error of at most 0.0003.
Values sent between devices are 32-bit elements; how exact they have to be, the bound alone decides.
No kernel may reach another device: no remote copies, remote signals or barrier semaphores. Data moves between devices by JAX's collectives and lax.ppermute only.
A program may use at most 320 MiB of HBM per device.

```python
import math
import jax
import jax.numpy as jnp
from jax import lax

M = 128
V = 4
NX = 256
NY = 256
PR = 2
BLOCK = 4
NOBS = 4096
OMAX = 128
STEPS = 3
CYCLES = 2
NS_ITERS = 10
P_SIZE = 128


def obs_layout(key):
    base = jax.random.fold_in(key, 7101)
    rows_blk = NX // BLOCK
    column_tiles = NY // BLOCK
    obs_index = jnp.arange(NOBS, dtype=jnp.int32)
    block_row = obs_index * rows_blk // NOBS
    block_col = jax.random.randint(jax.random.fold_in(base, 1), (NOBS,), 0, column_tiles)
    block_var = jax.random.randint(jax.random.fold_in(base, 2), (NOBS,), 0, V)
    block_col = jnp.where(obs_index == 0, 0, jnp.where(obs_index == NOBS - 1, column_tiles - 1, block_col))
    block_var = jnp.where(obs_index == 0, 0, jnp.where(obs_index == NOBS - 1, V - 1, block_var))
    tile_groups = (block_var * rows_blk + block_row) * column_tiles + block_col
    return (tile_groups.astype(jnp.int32), block_row.astype(jnp.int32))


def draw_obs_block(key, part):
    return obs_layout(key)[0]


def draw_readers(key, part):
    block_row = obs_layout(key)[1]
    rows_blk = NX // BLOCK
    patch_ids = jnp.arange(P_SIZE, dtype=jnp.int32)
    obs_index = jnp.arange(NOBS, dtype=jnp.int32)
    patch_row = (patch_ids * PR + PR // 2) // BLOCK
    row_gap = jnp.abs(block_row[None, :] - patch_row[:, None])
    distance = jnp.minimum(row_gap, rows_blk - row_gap)
    far_flag = (distance > 3).astype(jnp.int32)
    noise = jax.random.randint(jax.random.fold_in(key, 7202), (P_SIZE, NOBS), 0, 1 << 20)
    score = far_flag * (1 << 21) + noise
    planted = (patch_ids[:, None] == P_SIZE - 1) & (obs_index[None, :] == NOBS - 1) | (patch_ids[:, None] == 0) & (obs_index[None, :] == 0)
    score = jnp.where(planted, -1, score)
    order = jnp.argsort(score, axis=1, stable=True)
    return order[:, :OMAX].astype(jnp.int32)


def draw_counts(key, part):
    patch_ids = jnp.arange(P_SIZE, dtype=jnp.int32)
    drawn = jax.random.randint(jax.random.fold_in(key, 7303), (P_SIZE,), OMAX // 4, OMAX + 1)
    shuffled = jax.random.permutation(jax.random.fold_in(key, 7304), P_SIZE)
    drawn = jnp.where(patch_ids == shuffled[0], OMAX, jnp.where(patch_ids == shuffled[1], OMAX // 4, drawn))
    return drawn.astype(jnp.int32)


def steps_of(key, extent, pieces, smallest, high):
    gain, own = 1.0, jax.random.fold_in(key, 6)
    for position, parts in pieces:
        draws = jnp.exp(jax.random.uniform(jax.random.fold_in(own, position), (parts,), jnp.float32, smallest / len(pieces), high / len(pieces)))
        gain = gain * jnp.repeat(draws, extent[position] // parts).reshape([-1 if axis == position else 1 for axis in range(len(extent))])
    return gain


def gaussian(key, dims, scale, bound, cuts=(), kind=jnp.bfloat16):
    values = jax.random.normal(key, dims, jnp.float32) * scale
    if len(cuts) > 0:
        values = steps_of(key, dims, cuts, -0.22, 0.18) * values
    return jnp.clip(values, min=-bound, max=bound).astype(kind)


def setup_inputs(seed: int = 0) -> dict:
    streams_of = jax.random.split(jax.random.key(seed), 9)
    return {
        "ensemble": gaussian(streams_of[0], (M, V, NX, NY), 1.0, 6.0, ((0, 32),), jnp.float32),
        "flow_speed": gaussian(streams_of[1], (2, NX, NY), 0.2, 0.6, (), jnp.float32),
        "spreading_coefficient": jnp.clip(jnp.exp(jax.random.uniform(streams_of[2], (V, NX, NY), jnp.float32, math.log(0.01), math.log(0.12))), 0.01, 0.12),
        "obs_values": gaussian(streams_of[3], (CYCLES, NOBS), 1.0, 6.0, (), jnp.float32),
        "obs_var": jnp.clip(jnp.exp(jax.random.uniform(streams_of[4], (NOBS,), jnp.float32, math.log(0.02), math.log(0.5))), 0.02, 0.5),
        "obs_block": draw_obs_block(jax.random.fold_in(streams_of[8], 71), 0),
        "readers": draw_readers(jax.random.fold_in(streams_of[8], 71), 0),
        "counts": draw_counts(jax.random.fold_in(streams_of[8], 71), 0),
    }


EXACT_DOT = lax.Precision.HIGHEST
TAPER_ROWS = 6.0

def tendency(sample_ensemble, flow_speed, spreading_coefficient):
    shifted_up = jnp.roll(sample_ensemble, -1, axis=-2)
    shifted_down = jnp.roll(sample_ensemble, 1, axis=-2)
    shifted_left = jnp.roll(sample_ensemble, -1, axis=-1)
    shifted_right = jnp.roll(sample_ensemble, 1, axis=-1)
    advect_fields = flow_speed[0] * (shifted_up - shifted_down) * 0.5 + flow_speed[1] * (shifted_left - shifted_right) * 0.5
    return spreading_coefficient * (shifted_up + shifted_down + shifted_left + shifted_right - 4.0 * sample_ensemble) - advect_fields

def prior_guess(sample_ensemble, flow_speed, spreading_coefficient):
    for step in range(STEPS):
        section_one = sample_ensemble + tendency(sample_ensemble, flow_speed, spreading_coefficient)
        section_two = 0.75 * sample_ensemble + 0.25 * (section_one + tendency(section_one, flow_speed, spreading_coefficient))
        sample_ensemble = sample_ensemble / 3.0 + 2.0 / 3.0 * (section_two + tendency(section_two, flow_speed, spreading_coefficient))
    return sample_ensemble

def block_means(sample_ensemble):
    lead = sample_ensemble.shape[:-2]
    rows_sum = sample_ensemble.reshape(lead + (NX // BLOCK, BLOCK, NY)).sum(-2)
    column = jnp.arange(NY, dtype=jnp.int32) // BLOCK
    target_state = jnp.arange(NY // BLOCK, dtype=jnp.int32)
    pooling_matrix = (column[:, None] == target_state[None, :]).astype(jnp.float32)
    pooled = jnp.einsum('...c,cb->...b', rows_sum, pooling_matrix, precision=EXACT_DOT)
    return pooled.reshape(sample_ensemble.shape[0], -1) / (BLOCK * BLOCK)

def obs_weights(patch_index, chosen, obs_count, obs_block, obs_var):
    obs_blocks = obs_block[chosen]
    block_row = obs_blocks // (NY // BLOCK) % (NX // BLOCK)
    obs_row = block_row.astype(jnp.float32) * BLOCK + 0.5 * (BLOCK - 1)
    patch_row = patch_index.astype(jnp.float32) * PR + 0.5 * (PR - 1)
    row_gap = jnp.abs(obs_row - patch_row[..., None])
    distance = jnp.minimum(row_gap, NX - row_gap)
    taper = jnp.exp(-0.5 * (distance / TAPER_ROWS) ** 2)
    slot_index = jnp.arange(chosen.shape[-1], dtype=jnp.int32)
    in_list = slot_index < obs_count[..., None]
    return jnp.where(in_list, taper / obs_var[chosen], jnp.zeros_like(taper))

def analyse(patch_states, obs_rows, sensor_readings, weights):
    members = patch_states.shape[0]
    mean_state = patch_states.mean(0)
    pert = patch_states - mean_state
    hx_mean = obs_rows.mean(0)
    ypert = obs_rows - hx_mean
    innovation = sensor_readings - hx_mean
    identity = jnp.eye(members, dtype=jnp.float32)
    system = identity + jnp.dot(ypert * weights, ypert.T, precision=EXACT_DOT) / (members - 1)
    entrywise_magnitude = jnp.sqrt(jnp.sum(system * system))
    root_up = system / entrywise_magnitude
    inv_root = identity
    for sweep in range(NS_ITERS):
        newton = 1.5 * identity - 0.5 * jnp.dot(inv_root, root_up, precision=EXACT_DOT)
        root_up = jnp.dot(root_up, newton, precision=EXACT_DOT)
        inv_root = jnp.dot(newton, inv_root, precision=EXACT_DOT)
    obs_drive = jnp.dot(ypert, weights * innovation, precision=EXACT_DOT) / (members - 1)
    inner = jnp.dot(inv_root, obs_drive, precision=EXACT_DOT)
    mean_w = jnp.dot(inv_root, inner, precision=EXACT_DOT) / entrywise_magnitude
    transform = inv_root / jnp.sqrt(entrywise_magnitude) + mean_w[:, None]
    return mean_state + jnp.dot(transform.T, pert, precision=EXACT_DOT)

def reference(ensemble, flow_speed, spreading_coefficient, obs_values, obs_var, obs_block, readers, counts):
    sample_ensemble = ensemble
    for cycle in range(CYCLES):
        sample_ensemble = prior_guess(sample_ensemble, flow_speed, spreading_coefficient)
        model_obs = jnp.take(block_means(sample_ensemble), obs_block, axis=1)
        current = sample_ensemble

        def one_patch(patch_index):
            chosen = readers[patch_index]
            patch_states = lax.dynamic_slice_in_dim(current, patch_index * PR, PR, 2)
            weights = obs_weights(patch_index, chosen, counts[patch_index], obs_block, obs_var)
            updated = analyse(patch_states.reshape(M, V * PR * NY), jnp.take(model_obs, chosen, axis=1), obs_values[cycle][chosen], weights)
            return updated.reshape(M, V, PR, NY)
        stacked = lax.map(one_patch, jnp.arange(P_SIZE, dtype=jnp.int32))
        sample_ensemble = stacked.transpose(1, 2, 0, 3, 4).reshape(M, V, NX, NY)
    return sample_ensemble
```

```python
import functools

import jax
import jax.numpy as jnp
from jax import lax
from jax.experimental import pallas as pl
from jax.experimental.pallas import tpu as pltpu
from jax.sharding import PartitionSpec as P

PR = 2
BLOCK = 4
STEPS = 3
CYCLES = 2
NS_ITERS = 10
TAPER_ROWS = 6.0
HALO = 3 * STEPS
SUB = 8
MT = 16
F32 = jnp.float32
BF16 = jnp.bfloat16


def exact_dot(a, b):
    return jnp.dot(a, b, precision=lax.Precision.HIGHEST, preferred_element_type=F32)


def halves(x):
    hi = x.astype(BF16)
    return hi, (x - hi.astype(F32)).astype(BF16)


def thirds(x):
    hi = x.astype(BF16)
    rest = x - hi.astype(F32)
    mid = rest.astype(BF16)
    return hi, mid, (rest - mid.astype(F32)).astype(BF16)


def bdot(a, b):
    return jnp.dot(a, b, preferred_element_type=F32)


def dot3(a, b):
    (ah, al), (bh, bl) = a, b
    return bdot(ah, bh) + (bdot(ah, bl) + bdot(al, bh))


def member_forecast_kernel(
    owner_rows, q_ref, flow_ref, spread_ref, col_ref, var_ref, out_ref, hx_ref, coef, buf_q, buf_a, buf_b
):
    v = pl.program_id(0)
    nx, ny = buf_q.shape
    strips = nx // SUB
    sub = lax.broadcasted_iota(jnp.int32, (SUB, ny), 0)

    def rows(i):
        return pl.ds(pl.multiple_of(i * SUB, SUB), SUB)

    def fill(i, _):
        s = rows(i)
        sc = spread_ref[0, s, :]
        fx = 0.5 * flow_ref[0, s, :]
        fy = 0.5 * flow_ref[1, s, :]
        coef[0, s, :] = 1.0 - 4.0 * sc
        coef[1, s, :] = sc - fx
        coef[2, s, :] = sc + fx
        coef[3, s, :] = sc - fy
        coef[4, s, :] = sc + fy
        return 0

    lax.fori_loop(0, strips, fill, 0, unroll=2)

    def stage(src, write):
        def body(i, carry):
            cur, cur_up, prev_dn = carry
            nxt = src(lax.rem(i + 1, strips))
            nxt_up = pltpu.roll(nxt, SUB - 1, 0)
            cur_dn = pltpu.roll(cur, 1, 0)
            up = jnp.where(sub == SUB - 1, nxt_up, cur_up)
            dn = jnp.where(sub == 0, prev_dn, cur_dn)
            left = pltpu.roll(cur, ny - 1, 1)
            right = pltpu.roll(cur, 1, 1)
            s = rows(i)
            t = (
                coef[0, s, :] * cur
                + (coef[1, s, :] * up + coef[2, s, :] * dn)
                + (coef[3, s, :] * left + coef[4, s, :] * right)
            )
            write(s, t)
            return nxt, nxt_up, cur_dn

        first = src(0)
        lax.fori_loop(
            0,
            strips,
            body,
            (first, pltpu.roll(first, SUB - 1, 0), pltpu.roll(src(strips - 1), 1, 0)),
            unroll=4,
        )

    for step in range(STEPS):
        if step == 0:
            base = lambda s: q_ref[0, 0, s, :]
        else:
            base = lambda s: buf_q[s, :]

        def write_a(s, t):
            buf_a[s, :] = t

        def write_b(s, t, base=base):
            buf_b[s, :] = 0.75 * base(s) + 0.25 * t

        def write_q(s, t, base=base):
            buf_q[s, :] = base(s) * (1.0 / 3.0) + (2.0 / 3.0) * t

        stage(lambda i, base=base: base(rows(i)), write_a)
        stage(lambda i: buf_a[rows(i), :], write_b)
        stage(lambda i: buf_b[rows(i), :], write_q)

    height = out_ref.shape[2]
    for g, r in enumerate(owner_rows):
        out_ref[g, 0] = buf_q[r * height : (r + 1) * height, :]

    nbr, nbc = nx // BLOCK, ny // BLOCK
    lanes = hx_ref.shape[1]
    pool_rows = (
        lax.broadcasted_iota(jnp.int32, (nbr, nx), 1) // BLOCK
        == lax.broadcasted_iota(jnp.int32, (nbr, nx), 0)
    ).astype(F32)
    pool_cols = (
        lax.broadcasted_iota(jnp.int32, (ny, lanes), 0) // BLOCK
        == lax.broadcasted_iota(jnp.int32, (ny, lanes), 1)
    ).astype(F32)
    pooled = exact_dot(exact_dot(pool_rows, buf_q[...]), pool_cols) * (1.0 / (BLOCK * BLOCK))
    chosen = jnp.take_along_axis(pooled, col_ref[...], axis=1, mode="promise_in_bounds")
    chosen = jnp.where(var_ref[...] == v, chosen, 0.0)

    @pl.when(v == 0)
    def _():
        hx_ref[...] = chosen

    @pl.when(v > 0)
    def _():
        hx_ref[...] += chosen


def member_forecast(j, ensemble, flow, spread, col, var, owner_rows):
    _, nv, nx, ny = ensemble.shape
    groups = len(owner_rows)
    height = nx // groups
    return pl.pallas_call(
        functools.partial(member_forecast_kernel, owner_rows),
        grid=(nv,),
        in_specs=[
            pl.BlockSpec((1, 1, nx, ny), lambda v: (j, v, 0, 0)),
            pl.BlockSpec((2, nx, ny), lambda v: (0, 0, 0)),
            pl.BlockSpec((1, nx, ny), lambda v: (v, 0, 0)),
            pl.BlockSpec(col.shape, lambda v: (0, 0)),
            pl.BlockSpec(var.shape, lambda v: (0, 0)),
        ],
        out_specs=[
            pl.BlockSpec((groups, 1, height, ny), lambda v: (0, v, 0, 0)),
            pl.BlockSpec(col.shape, lambda v: (0, 0)),
        ],
        out_shape=[
            jax.ShapeDtypeStruct((groups, nv, height, ny), F32),
            jax.ShapeDtypeStruct(col.shape, F32),
        ],
        scratch_shapes=[pltpu.VMEM((5, nx, ny), F32)] + [pltpu.VMEM((nx, ny), F32)] * 3,
        name="member_forecast",
    )(ensemble, flow, spread, col, var)


def transform_kernel(base_ref, hx_ref, chosen_ref, weight_ref, value_ref, out_ref):
    blocks, members, width = hx_ref.shape
    count, _, slots = chosen_ref.shape
    chosen = jnp.concatenate([chosen_ref[p] for p in range(count)], axis=1)
    row = lax.broadcasted_iota(jnp.int32, (width, count * slots), 0)

    def gather(b, acc):
        pick = (row + base_ref[b] == chosen).astype(F32).astype(BF16)
        hi, mid, lo = thirds(hx_ref[b])
        return acc + (bdot(hi, pick) + (bdot(mid, pick) + bdot(lo, pick)))

    hx = lax.fori_loop(0, blocks, gather, jnp.zeros((members, count * slots), F32))
    eye = (
        lax.broadcasted_iota(jnp.int32, (members, members), 0)
        == lax.broadcasted_iota(jnp.int32, (members, members), 1)
    ).astype(F32)
    scale = 1.0 / (members - 1)
    roots, drives, norms = [], [], []
    for p in range(count):
        part = hx[:, p * slots : (p + 1) * slots]
        mean = jnp.mean(part, axis=0, keepdims=True)
        y = part - mean
        w = weight_ref[p]
        gram = lax.dot_general(
            y * w, y, (((1,), (1,)), ((), ())), precision=lax.Precision.HIGHEST, preferred_element_type=F32
        )
        system = eye + gram * scale
        norm = jnp.sqrt(jnp.sum(system * system, keepdims=True))
        roots.append(system / norm)
        norms.append(norm)
        drive = jnp.sum(y * (w * (value_ref[p] - mean)), axis=1, keepdims=True) * scale
        drives.append(jnp.broadcast_to(drive, (members, members)))
    inverses = [None] * count
    for sweep in range(NS_ITERS):
        for p in range(count):
            s = halves(roots[p])
            if sweep == 0:
                newton = 1.5 * eye - 0.5 * roots[p]
                inverses[p] = newton
                n = halves(newton)
            else:
                z = halves(inverses[p])
                newton = 1.5 * eye - 0.5 * dot3(z, s)
                n = halves(newton)
                inverses[p] = dot3(n, z)
            if sweep < NS_ITERS - 1:
                roots[p] = dot3(s, n)
    for p in range(count):
        z = halves(inverses[p])
        mean_w = dot3(z, halves(dot3(z, halves(drives[p])))) / norms[p]
        out_ref[p] = inverses[p] / jnp.sqrt(norms[p]) + mean_w


def transforms(base, hx, chosen, weight, value):
    blocks, members, width = hx.shape
    count = chosen.shape[0]
    return pl.pallas_call(
        transform_kernel,
        in_specs=[pl.BlockSpec(memory_space=pltpu.SMEM)] + [pl.BlockSpec(memory_space=pltpu.VMEM)] * 4,
        out_specs=pl.BlockSpec(memory_space=pltpu.VMEM),
        out_shape=jax.ShapeDtypeStruct((count, members, members), F32),
        name="transforms",
    )(base, hx, chosen, weight, value)


def mix(transform, x):
    mean = jnp.mean(x, axis=0, keepdims=True)
    gh, gl = halves(transform.T)
    return mean + dot3((gh, gl), halves(x - mean))


def first_analysis_kernel(count, q_ref, g_ref, *refs):
    parts, out_ref = refs[:-1], refs[-1]
    tile = pl.program_id(0)
    for p in range(SUB // PR):
        patch = tile * (SUB // PR) + p
        g = g_ref[lax.bitwise_xor(patch // count, q_ref[0]), lax.rem(patch, count)]
        x = jnp.concatenate(
            [jnp.concatenate([part[:, PR * p + i, :] for part in parts], axis=0) for i in range(PR)], axis=1
        )
        y = mix(g, x)
        ny = parts[0].shape[2]
        for i in range(PR):
            out_ref[PR * p + i] = y[:, i * ny : (i + 1) * ny]


def first_analysis(q, g, parts):
    n, height, ny = parts[0].shape
    members = n * len(parts)
    return pl.pallas_call(
        functools.partial(first_analysis_kernel, g.shape[1]),
        grid=(height // SUB,),
        in_specs=[
            pl.BlockSpec(memory_space=pltpu.SMEM),
            pl.BlockSpec(g.shape, lambda i: (0, 0, 0, 0)),
        ]
        + [pl.BlockSpec((n, SUB, ny), lambda i: (0, i, 0))] * len(parts),
        out_specs=pl.BlockSpec((SUB, members, ny), lambda i: (i, 0, 0)),
        out_shape=jax.ShapeDtypeStruct((height, members, ny), F32),
        name="first_analysis",
    )(q, g, *parts)


def last_analysis_kernel(count, q_ref, g_ref, x_ref, *outs):
    tile = pl.program_id(0)
    n = outs[0].shape[0]
    ny = x_ref.shape[2]
    for p in range(SUB // PR):
        patch = tile * (SUB // PR) + p
        g = g_ref[lax.bitwise_xor(patch // count, q_ref[0]), lax.rem(patch, count)]
        x = jnp.concatenate([x_ref[PR * p + i] for i in range(PR)], axis=1)
        y = mix(g, x)
        for i in range(PR):
            for j, out in enumerate(outs):
                out[:, PR * p + i, :] = y[j * n : (j + 1) * n, i * ny : (i + 1) * ny]


def last_analysis(q, g, x, pieces):
    height, members, ny = x.shape
    n = members // pieces
    return pl.pallas_call(
        functools.partial(last_analysis_kernel, g.shape[1]),
        grid=(height // SUB,),
        in_specs=[
            pl.BlockSpec(memory_space=pltpu.SMEM),
            pl.BlockSpec(g.shape, lambda i: (0, 0, 0, 0)),
            pl.BlockSpec((SUB, members, ny), lambda i: (i, 0, 0)),
        ],
        out_specs=[pl.BlockSpec((n, SUB, ny), lambda i: (0, i, 0))] * pieces,
        out_shape=[jax.ShapeDtypeStruct((n, height, ny), F32)] * pieces,
        name="last_analysis",
    )(q, g, x)


def group_forecast_kernel(x_ref, lo_ref, hi_ref, coef_ref, pick_ref, out_ref, hx_ref, buf_q, buf_a, buf_b):
    height, mt, ny = x_ref.shape
    halo = lo_ref.shape[0]
    total = height + 2 * halo
    buf_q[:halo] = lo_ref[...]
    buf_q[halo : halo + height] = x_ref[...]
    buf_q[halo + height :] = hi_ref[...]

    def stage(src, lo, hi, write):
        def body(i, carry):
            prev, cur = carry
            nxt = src[i + 1]
            left = pltpu.roll(cur, ny - 1, 1)
            right = pltpu.roll(cur, 1, 1)
            k = [jnp.concatenate([coef_ref[c, i]] * (mt // SUB), axis=0) for c in range(5)]
            t = k[0] * cur + (k[1] * nxt + k[2] * prev) + (k[3] * left + k[4] * right)
            write(i, t)
            return cur, nxt

        lax.fori_loop(lo, hi, body, (src[lo - 1], src[lo]), unroll=2)

    def write_a(i, t):
        buf_a[i] = t

    def write_b(i, t):
        buf_b[i] = 0.75 * buf_q[i] + 0.25 * t

    def write_q(i, t):
        buf_q[i] = buf_q[i] * (1.0 / 3.0) + (2.0 / 3.0) * t

    for step in range(STEPS):
        e = 3 * step
        stage(buf_q, e + 1, total - e - 1, write_a)
        stage(buf_a, e + 2, total - e - 2, write_b)
        stage(buf_b, e + 3, total - e - 3, write_q)

    out_ref[...] = buf_q[halo : halo + height]
    block_rows = height // BLOCK
    per = pick_ref.shape[2]
    for b in range(block_rows):
        at = halo + BLOCK * b
        total_rows = (buf_q[at] + buf_q[at + 1]) + (buf_q[at + 2] + buf_q[at + 3])
        hi, mid, lo = thirds(total_rows)
        pick = pick_ref[b]
        hx_ref[:, b * per : (b + 1) * per] = bdot(hi, pick) + (bdot(mid, pick) + bdot(lo, pick))


def group_forecast(x, lo, hi, coef, pick):
    height, members, ny = x.shape
    halo = lo.shape[0]
    total = height + 2 * halo
    width = pick.shape[0] * pick.shape[2]
    return pl.pallas_call(
        group_forecast_kernel,
        grid=(members // MT,),
        in_specs=[
            pl.BlockSpec((height, MT, ny), lambda i: (0, i, 0)),
            pl.BlockSpec((halo, MT, ny), lambda i: (0, i, 0)),
            pl.BlockSpec((halo, MT, ny), lambda i: (0, i, 0)),
            pl.BlockSpec(coef.shape, lambda i: (0, 0, 0, 0)),
            pl.BlockSpec(pick.shape, lambda i: (0, 0, 0)),
        ],
        out_specs=[
            pl.BlockSpec((height, MT, ny), lambda i: (0, i, 0)),
            pl.BlockSpec((MT, width), lambda i: (i, 0)),
        ],
        out_shape=[
            jax.ShapeDtypeStruct((height, members, ny), F32),
            jax.ShapeDtypeStruct((members, width), F32),
        ],
        scratch_shapes=[pltpu.VMEM((total, MT, ny), F32)] * 3,
        name="group_forecast",
    )(x, lo, hi, coef, pick)


def local(n, ensemble, flow_speed, spreading, obs_values, obs_var, obs_block, readers, counts):
    mine, nv, nx, ny = ensemble.shape
    members = mine * n
    nobs = obs_var.shape[0]
    patches, slots = readers.shape
    groups = n // nv
    height = nx // groups
    count = patches // n
    width = nobs // n
    nbr, nbc = nx // BLOCK, ny // BLOCK
    per_row = nobs // nbr

    place = [2 * r if 2 * r < groups else 2 * (groups - 1 - r) + 1 for r in range(groups)]
    owner_rows = [place.index(g) for g in range(groups)]

    def device(r, q):
        return nv * place[r % groups] + q

    me = lax.axis_index("dev")
    q = lax.rem(me, nv)
    g = me // nv
    r = jnp.where(g % 2 == 0, g // 2, groups - 1 - g // 2) if groups > 1 else g * 0
    spot = r * nv + q
    q_ref = q.reshape(1).astype(jnp.int32)

    obs_col = obs_block % nbc
    obs_v = obs_block // (nbr * nbc)
    lanes = max(128, nbc)
    col_table = jnp.pad(obs_col.reshape(nbr, per_row), ((0, 0), (0, lanes - per_row)))
    var_table = jnp.pad(obs_v.reshape(nbr, per_row), ((0, 0), (0, lanes - per_row)))

    first = spot * count
    chosen = lax.dynamic_slice_in_dim(readers, first, count, 0)
    my_counts = lax.dynamic_slice_in_dim(counts, first, count, 0)
    patch_index = first + jnp.arange(count, dtype=jnp.int32)
    obs_row = (chosen * nbr // nobs).astype(F32) * BLOCK + 0.5 * (BLOCK - 1)
    patch_row = patch_index.astype(F32) * PR + 0.5 * (PR - 1)
    gap = jnp.abs(obs_row - patch_row[:, None])
    distance = jnp.minimum(gap, nx - gap)
    taper = jnp.exp(-0.5 * (distance / TAPER_ROWS) ** 2)
    listed = jnp.arange(slots, dtype=jnp.int32) < my_counts[:, None]
    weight = jnp.where(listed, taper / obs_var[chosen], 0.0)[:, None, :]
    chosen_rows = chosen[:, None, :]

    rows = lax.rem(r * height - HALO + jnp.arange(height + 2 * HALO, dtype=jnp.int32) + nx, nx)
    doubled = lambda a: jnp.concatenate([a, a, a], axis=-2)
    start = r * height - HALO + nx
    take = lambda a: lax.dynamic_slice_in_dim(doubled(a), start, height + 2 * HALO, a.ndim - 2)
    my_flow = 0.5 * take(flow_speed)
    my_spread = take(lax.dynamic_index_in_dim(spreading, q, 0, keepdims=False))
    coef = jnp.stack(
        [
            1.0 - 4.0 * my_spread,
            my_spread - my_flow[0],
            my_spread + my_flow[0],
            my_spread - my_flow[1],
            my_spread + my_flow[1],
        ]
    )
    coef = jnp.broadcast_to(coef[:, :, None, :], coef.shape[:2] + (SUB, ny))
    block_rows = height // BLOCK
    group_col = lax.dynamic_slice_in_dim(obs_col.reshape(nbr, per_row), r * block_rows, block_rows, 0)
    group_var = lax.dynamic_slice_in_dim(obs_v.reshape(nbr, per_row), r * block_rows, block_rows, 0)
    column = jnp.arange(ny, dtype=jnp.int32) // BLOCK
    pick = jnp.where(
        (column[None, :, None] == group_col[:, None, :]) & (group_var[:, None, :] == q),
        1.0 / (BLOCK * BLOCK),
        0.0,
    ).astype(BF16)

    def solve(cycle, hx):
        every = lax.all_to_all(jnp.broadcast_to(hx[None], (n,) + hx.shape), "dev", 0, 0, tiled=True)
        base = jnp.array([(owner_rows[d // nv] * nv + d % nv) * width for d in range(n)], jnp.int32)
        value = obs_values[cycle][chosen][:, None, :]
        own = transforms(base, every, chosen_rows, weight, value)
        stacked = [own]
        for c in range(1, nv):
            pairs = [(nv * b + i, nv * b + (i ^ c)) for b in range(groups) for i in range(nv)]
            stacked.append(lax.ppermute(own, "dev", pairs))
        return jnp.stack(stacked)

    arrived, observed = [], []
    for j in range(mine):
        fields, hx = member_forecast(j, ensemble, flow_speed, spreading, col_table, var_table, owner_rows)
        arrived.append(lax.all_to_all(fields.reshape(n, height, ny), "dev", 0, 0, tiled=True))
        observed.append(hx[:, :per_row].reshape(groups, nv, width))
    observed = jnp.stack(observed, 2)
    observed = jnp.concatenate([observed[r0 : r0 + 1] for r0 in owner_rows], 0).reshape(n, mine, width)
    observed = lax.all_to_all(observed, "dev", 0, 0, tiled=True)
    hx = observed.transpose(1, 0, 2).reshape(members, width)
    state = first_analysis(q_ref, solve(0, hx), arrived)

    lo, hi = [], []
    left = HALO
    hop = 1
    while left > 0:
        rows_k = min(left, height)
        up = [(device(r0, i), device(r0 + hop, i)) for r0 in range(groups) for i in range(nv)]
        down = [(b, a) for a, b in up]
        lo.insert(0, lax.ppermute(state[height - rows_k :], "dev", up))
        hi.append(lax.ppermute(state[:rows_k], "dev", down))
        left -= rows_k
        hop += 1
    lo = lo[0] if len(lo) == 1 else jnp.concatenate(lo, 0)
    hi = hi[0] if len(hi) == 1 else jnp.concatenate(hi, 0)
    state, partial = group_forecast(state, lo, hi, coef, pick)
    partial = partial.reshape(members, nv, width)
    pieces = [lax.dynamic_index_in_dim(partial, q, 1, keepdims=False)]
    for c in range(1, nv):
        pairs = [(nv * b + i, nv * b + (i ^ c)) for b in range(groups) for i in range(nv)]
        other = lax.dynamic_index_in_dim(partial, lax.bitwise_xor(q, c), 1, keepdims=False)
        pieces.append(lax.ppermute(other, "dev", pairs))
    hx = functools.reduce(lambda a, b: a + b, pieces)
    outs = last_analysis(q_ref, solve(1, hx), state, mine)
    final = []
    for out in outs:
        back = lax.all_to_all(out, "dev", 0, 0, tiled=True).reshape(groups, nv, height, ny)
        back = jnp.concatenate([back[place[r0]][:, None] for r0 in range(groups)], 1)
        final.append(back.reshape(nv, nx, ny))
    return jnp.stack(final)


def solution(mesh):
    n = mesh.shape["dev"]
    return jax.shard_map(
        functools.partial(local, n),
        mesh=mesh,
        in_specs=(P("dev", None, None, None), P(), P(), P(), P(), P(), P(), P()),
        out_specs=P("dev", None, None, None),
        check_vma=False,
    )
```

```python
import functools

import jax
import jax.numpy as jnp
from jax import lax
from jax.experimental import pallas as pl
from jax.experimental.pallas import tpu as pltpu
from jax.sharding import PartitionSpec as P

PR = 2
BLOCK = 4
STEPS = 3
CYCLES = 2
NS_ITERS = 10
TAPER_ROWS = 6.0
HALO = 3 * STEPS
SUB = 8
NEAR = 3
SCALES = (1.0 / 3.0, 0.5, 1.0)
F32 = jnp.float32
BF16 = jnp.bfloat16


def exact_dot(a, b):
    return jnp.dot(a, b, precision=lax.Precision.HIGHEST, preferred_element_type=F32)


def halves(x):
    hi = x.astype(BF16)
    return hi, (x - hi.astype(F32)).astype(BF16)


def thirds(x):
    hi = x.astype(BF16)
    rest = x - hi.astype(F32)
    mid = rest.astype(BF16)
    return hi, mid, (rest - mid.astype(F32)).astype(BF16)


def bdot(a, b):
    return jnp.dot(a, b, preferred_element_type=F32)


def dot3(a, b):
    (ah, al), (bh, bl) = a, b
    return bdot(ah, bh) + (bdot(ah, bl) + bdot(al, bh))


def stencil(src, base, coef, at, lo, hi, rb, unroll, write):
    copies = src.shape[1] // SUB
    half = src.shape[2] // 2

    def k(c, rows):
        v = coef[at + c, rows]
        return v if copies == 1 else jnp.concatenate([v] * copies, axis=1)

    def body(t, _):
        i = lo + t * rb
        rows = pl.ds(i, rb)
        x = src[pl.ds(i - 1, rb + 2)]
        cur, up, dn = x[1:-1], x[2:], x[:-2]
        even, odd = cur[..., :half], cur[..., half:]
        left = jnp.concatenate([odd, pltpu.roll(even, half - 1, 2)], axis=2)
        right = jnp.concatenate([pltpu.roll(odd, 1, 2), even], axis=2)
        total = (k(0, rows) * cur + (k(1, rows) * up + k(2, rows) * dn)) + (
            k(3, rows) * left + k(4, rows) * right
        )
        write[rows] = total if base is None else base[rows] + total
        return 0

    n = -(-(hi - lo) // rb)
    lax.fori_loop(0, n, body, 0, unroll=min(unroll, n))


def store_coefs(coef, rows, spread, fx, fy):
    parts = (-4.0 * spread, spread - fx, spread + fx, spread - fy, spread + fy)
    for s, scale in enumerate(SCALES):
        for c, part in enumerate(parts):
            v = part if scale == 1.0 else scale * part
            coef[5 * s + c, rows] = 1.0 + v if (s == 0 and c == 0) else v


def lane_gather(x, idx):
    return jnp.take_along_axis(x, idx, axis=1, mode="promise_in_bounds")


def strided(nat, t, t_rows):
    a, b = (nat[h, pl.ds(t, SUB, stride=t_rows), :] for h in range(2))
    half = a.shape[1]
    lane = lax.broadcasted_iota(jnp.int32, a.shape, 1)
    idx = lax.rem(2 * lane, half)
    low = lane < half // 2
    return jnp.concatenate(
        [jnp.where(low, lane_gather(a, idx + i), lane_gather(b, idx + i)) for i in range(2)], axis=1
    )


def interleave(x):
    half = x.shape[1] // 2
    even, odd = x[:, :half], x[:, half:]
    lane = lax.broadcasted_iota(jnp.int32, even.shape, 1)
    is_even = lax.rem(lane, 2) == 0
    idx = lane // 2
    return jnp.concatenate(
        [
            jnp.where(is_even, lane_gather(even, idx + h * (half // 2)), lane_gather(odd, idx + h * (half // 2)))
            for h in range(2)
        ],
        axis=1,
    )


def lay(nat, field):
    half = nat.shape[2]
    for h in range(2):
        nat[h] = field[:, h * half : (h + 1) * half]


def member_kernel(
    owner_rows, rb, unroll, q_ref, flow_ref, spread_ref, col_ref, var_ref, out_ref, hx_ref, coef, flow, buf_q, buf_a, buf_b, nat, sums
):
    v = pl.program_id(0)
    many = q_ref.shape[0]
    nv = sums.shape[1]
    nx, ny = q_ref.shape[2:]
    half = ny // 2
    t_rows = nx // SUB

    @pl.when(v == 0)
    def _():
        for c in range(2):
            lay(nat, flow_ref[c])

            def fill(t, _, c=c):
                flow[c, t] = 0.5 * strided(nat, t, t_rows)
                return 0

            lax.fori_loop(0, t_rows, fill, 0, unroll=8)

    lay(nat, spread_ref[0])

    def fill(t, _):
        store_coefs(coef, pl.ds(t + 1, 1), strided(nat, t, t_rows)[None], flow[0, pl.ds(t, 1)], flow[1, pl.ds(t, 1)])
        return 0

    lax.fori_loop(0, t_rows, fill, 0, unroll=8)
    for j in range(many):
        lay(nat, q_ref[j, 0])

        def fill(t, _, j=j):
            buf_q[t + 1, j * SUB : (j + 1) * SUB] = strided(nat, t, t_rows)
            return 0

        lax.fori_loop(0, t_rows, fill, 0, unroll=8)

    def wrap(buf):
        for j in range(many):
            s = slice(j * SUB, (j + 1) * SUB)
            buf[0, s] = pltpu.roll(buf[t_rows, s], 1, 0)
            buf[t_rows + 1, s] = pltpu.roll(buf[1, s], SUB - 1, 0)

    for step in range(STEPS):
        wrap(buf_q)
        stencil(buf_q, None, coef, 0, 1, t_rows + 1, rb, unroll, buf_a)
        wrap(buf_a)
        stencil(buf_a, buf_q, coef, 5, 1, t_rows + 1, rb, unroll, buf_b)
        wrap(buf_b)
        stencil(buf_b, buf_q, coef, 10, 1, t_rows + 1, rb, unroll, buf_q)

    height = out_ref.shape[3]
    per = t_rows // BLOCK * SUB
    for j in range(many):
        s = slice(j * SUB, (j + 1) * SUB)

        def put(t, _, s=s):
            for h in range(2):
                nat[h, pl.ds(t, SUB, stride=t_rows), :] = buf_q[t + 1, s, h * half : (h + 1) * half]
            return 0

        lax.fori_loop(0, t_rows, put, 0, unroll=8)
        for g, r in enumerate(owner_rows):
            for h in range(2):
                out_ref[g, 0, j, :, h * half : (h + 1) * half] = nat[h, r * height : (r + 1) * height, :]
        x = buf_q[1 : t_rows + 1, s].reshape(t_rows // BLOCK, BLOCK, SUB, ny)
        sums[j, v] = ((x[:, 0] + x[:, 1]) + (x[:, 2] + x[:, 3])).reshape(per, ny)

    @pl.when(v == nv - 1)
    def _():
        lanes = hx_ref.shape[2]
        column = lax.rem(lax.broadcasted_iota(jnp.int32, (ny, lanes), 0), half) // (BLOCK // 2)
        pool = (column == lax.broadcasted_iota(jnp.int32, (ny, lanes), 1)).astype(F32)
        pooled = exact_dot(sums[...].reshape(many * nv * per, ny), pool) * (1.0 / (BLOCK * BLOCK))
        for j in range(many):
            total = jnp.zeros((per, lanes), F32)
            for w in range(nv):
                at = (j * nv + w) * per
                chosen = lane_gather(pooled[at : at + per], col_ref[...])
                total = total + jnp.where(var_ref[...] == w, chosen, 0.0)
            hx_ref[j] = total


def member_forecast(first, many, ensemble, flow, spread, col, var, owner_rows):
    _, nv, nx, ny = ensemble.shape
    groups = len(owner_rows)
    height, t_rows = nx // groups, nx // SUB
    rb, unroll = (16, 2) if many == 1 else (8, 4)
    part = ensemble if many == ensemble.shape[0] else lax.slice_in_dim(ensemble, first, first + many, axis=0)
    return pl.pallas_call(
        functools.partial(member_kernel, owner_rows, rb, unroll),
        grid=(nv,),
        in_specs=[
            pl.BlockSpec((many, 1, nx, ny), lambda v: (0, v, 0, 0)),
            pl.BlockSpec((2, nx, ny), lambda v: (0, 0, 0)),
            pl.BlockSpec((1, nx, ny), lambda v: (v, 0, 0)),
            pl.BlockSpec(col.shape, lambda v: (0, 0)),
            pl.BlockSpec(var.shape, lambda v: (0, 0)),
        ],
        out_specs=[
            pl.BlockSpec((groups, 1, many, height, ny), lambda v: (0, v, 0, 0, 0)),
            pl.BlockSpec((many,) + col.shape, lambda v: (0, 0, 0)),
        ],
        out_shape=[
            jax.ShapeDtypeStruct((groups, nv, many, height, ny), F32),
            jax.ShapeDtypeStruct((many,) + col.shape, F32),
        ],
        scratch_shapes=[
            pltpu.VMEM((15, t_rows + 2, SUB, ny), F32),
            pltpu.VMEM((2, t_rows, SUB, ny), F32),
        ]
        + [pltpu.VMEM((t_rows + 2, many * SUB, ny), F32)] * 3
        + [pltpu.VMEM((2, nx, ny // 2), F32), pltpu.VMEM((many, nv, nx // BLOCK, ny), F32)],
        name=f"member_forecast_{many}",
    )(part, flow, spread, col, var)


def group_kernel(rb, unroll, x_ref, lo_ref, hi_ref, raw_ref, pick_ref, out_ref, hx_ref, coef, buf_q, buf_a, buf_b):
    height, _, ny = x_ref.shape
    halo = lo_ref.shape[0]
    total = height + 2 * halo

    @pl.when(pl.program_id(0) == 0)
    def _():
        def fill(i, _):
            rows = pl.ds(i, 1)
            store_coefs(coef, rows, raw_ref[0, rows], raw_ref[1, rows], raw_ref[2, rows])
            return 0

        lax.fori_loop(0, total, fill, 0, unroll=2)

    buf_q[:halo] = lo_ref[...]
    buf_q[halo : halo + height] = x_ref[...]
    buf_q[halo + height : total] = hi_ref[...]
    for step in range(STEPS):
        e = 3 * step
        stencil(buf_q, None, coef, 0, e + 1, total - e - 1, rb, unroll, buf_a)
        stencil(buf_a, buf_q, coef, 5, e + 2, total - e - 2, rb, unroll, buf_b)
        stencil(buf_b, buf_q, coef, 10, e + 3, total - e - 3, rb, unroll, buf_q)

    out_ref[...] = buf_q[halo : halo + height]
    per = pick_ref.shape[2]
    for b in range(height // BLOCK):
        at = halo + BLOCK * b
        rows_sum = (buf_q[at] + buf_q[at + 1]) + (buf_q[at + 2] + buf_q[at + 3])
        hi, mid, lo = thirds(rows_sum)
        pick = pick_ref[b]
        hx_ref[:, b * per : (b + 1) * per] = bdot(hi, pick) + (bdot(mid, pick) + bdot(lo, pick))


def group_forecast(first, mt, x, lo, hi, raw, pick):
    height, _, ny = x.shape
    halo, many = lo.shape[:2]
    total = height + 2 * halo
    width = pick.shape[0] * pick.shape[2]
    rb, unroll = 2, 4
    skip = first * (many // mt)
    return pl.pallas_call(
        functools.partial(group_kernel, rb, unroll),
        grid=(many // mt,),
        in_specs=[
            pl.BlockSpec((height, mt, ny), lambda i: (0, i + skip, 0)),
            pl.BlockSpec((halo, mt, ny), lambda i: (0, i, 0)),
            pl.BlockSpec((halo, mt, ny), lambda i: (0, i, 0)),
            pl.BlockSpec(raw.shape, lambda i: (0, 0, 0, 0)),
            pl.BlockSpec(pick.shape, lambda i: (0, 0, 0)),
        ],
        out_specs=[
            pl.BlockSpec((height, mt, ny), lambda i: (0, i, 0)),
            pl.BlockSpec((mt, width), lambda i: (i, 0)),
        ],
        out_shape=[
            jax.ShapeDtypeStruct((height, many, ny), F32),
            jax.ShapeDtypeStruct((many, width), F32),
        ],
        scratch_shapes=[pltpu.VMEM((15, total + rb * unroll, SUB, ny), F32)]
        + [pltpu.VMEM((total + rb * unroll, mt, ny), F32)] * 3,
        name="group_forecast",
    )(x, lo, hi, raw, pick)


def select_kernel(base_ref, chosen_ref, *refs):
    blocks, out_ref = refs[:-1], refs[-1]
    width = blocks[0].shape[2]
    count, _, slots = chosen_ref.shape
    chosen = jnp.concatenate([chosen_ref[p] for p in range(count)], axis=1)
    row = lax.broadcasted_iota(jnp.int32, (width, count * slots), 0)

    def part(block, base):
        pick = (row + base == chosen).astype(F32).astype(BF16)
        hi, mid, lo = thirds(block)
        return bdot(hi, pick) + (bdot(mid, pick) + bdot(lo, pick))

    if len(blocks) == 1:
        only = blocks[0]
        out_ref[...] = lax.fori_loop(
            0,
            only.shape[0],
            lambda b, acc: acc + part(only[b], base_ref[b]),
            jnp.zeros(out_ref.shape, F32),
        )
    else:
        total = part(blocks[0][0], base_ref[0])
        for b in range(1, len(blocks)):
            total = total + part(blocks[b][0], base_ref[b])
        out_ref[...] = total


def select(base, chosen, blocks):
    members = blocks[0].shape[1]
    return pl.pallas_call(
        select_kernel,
        in_specs=[pl.BlockSpec(memory_space=pltpu.SMEM)]
        + [pl.BlockSpec(memory_space=pltpu.VMEM)] * (1 + len(blocks)),
        out_specs=pl.BlockSpec(memory_space=pltpu.VMEM),
        out_shape=jax.ShapeDtypeStruct((members, chosen.shape[0] * chosen.shape[2]), F32),
        name="select",
    )(base, chosen, *blocks)


def transform_kernel(hx_ref, weight_ref, value_ref, out_ref):
    members = hx_ref.shape[0]
    count, _, slots = weight_ref.shape
    eye = (
        lax.broadcasted_iota(jnp.int32, (members, members), 0)
        == lax.broadcasted_iota(jnp.int32, (members, members), 1)
    ).astype(F32)
    scale = 1.0 / (members - 1)
    roots, drives, norms = [], [], []
    for p in range(count):
        part = hx_ref[:, p * slots : (p + 1) * slots]
        mean = jnp.mean(part, axis=0, keepdims=True)
        y = part - mean
        w = weight_ref[p]
        gram = lax.dot_general(
            y * w, y, (((1,), (1,)), ((), ())), precision=lax.Precision.HIGHEST, preferred_element_type=F32
        )
        system = eye + gram * scale
        norm = jnp.sqrt(jnp.sum(system * system, keepdims=True))
        roots.append(system / norm)
        norms.append(norm)
        drive = jnp.sum(y * (w * (value_ref[p] - mean)), axis=1, keepdims=True) * scale
        drives.append(jnp.broadcast_to(drive, (members, members)))
    inverses = [None] * count
    for sweep in range(NS_ITERS):
        for p in range(count):
            s = halves(roots[p])
            if sweep == 0:
                newton = 1.5 * eye - 0.5 * roots[p]
                inverses[p] = newton
                n = halves(newton)
            else:
                z = halves(inverses[p])
                newton = 1.5 * eye - 0.5 * dot3(z, s)
                n = halves(newton)
                inverses[p] = dot3(n, z)
            if sweep < NS_ITERS - 1:
                roots[p] = dot3(s, n)
    for p in range(count):
        z = halves(inverses[p])
        mean_w = dot3(z, halves(dot3(z, halves(drives[p])))) / norms[p]
        out_ref[p] = inverses[p] / jnp.sqrt(norms[p]) + mean_w


def transforms(hx, weight, value):
    members = hx.shape[0]
    return pl.pallas_call(
        transform_kernel,
        in_specs=[pl.BlockSpec(memory_space=pltpu.VMEM)] * 3,
        out_specs=pl.BlockSpec(memory_space=pltpu.VMEM),
        out_shape=jax.ShapeDtypeStruct((weight.shape[0], members, members), F32),
        name="transforms",
    )(hx, weight, value)


def mix(transform, x):
    mean = jnp.mean(x, axis=0, keepdims=True)
    return mean + dot3(halves(transform.T), halves(x - mean))


def first_analysis_kernel(count, nparts, chunks, q_ref, *refs):
    gs, parts, outs = refs[: len(refs) - nparts - 1 - 2 * chunks], refs[-nparts - 1 - 2 * chunks : -1 - 2 * chunks], refs[-1 - 2 * chunks :]
    out_ref, sends = outs[0], outs[1:]
    tile = pl.program_id(0)
    ny = out_ref.shape[2]
    for p in range(SUB // PR):
        patch = tile * (SUB // PR) + p
        g = gs[0][lax.bitwise_xor(patch // count, q_ref[0]), lax.rem(patch, count)]
        x = jnp.concatenate(
            [
                jnp.concatenate(
                    [part[:, j, PR * p + i, :] for part in parts for j in range(part.shape[1])], axis=0
                )
                for i in range(PR)
            ],
            axis=1,
        )
        y = mix(g, x)
        for i in range(PR):
            out_ref[PR * p + i] = y[:, i * ny : (i + 1) * ny]
    if chunks:
        halo, many = sends[0].shape[:2]
        height = SUB * pl.num_programs(0)
        tiles = -(-halo // SUB)
        for c in range(chunks):
            lo, hi = sends[2 * c], sends[2 * c + 1]
            members = slice(c * many, (c + 1) * many)
            for k in range(tiles):

                @pl.when(tile == k)
                def _():
                    rows = min(SUB, halo - SUB * k)
                    hi[SUB * k : SUB * k + rows] = out_ref[:rows, members]

                @pl.when(tile == pl.num_programs(0) - 1 - k)
                def _():
                    rows = min(SUB, halo - SUB * k)
                    lo[halo - SUB * k - rows : halo - SUB * k] = out_ref[SUB - rows :, members]


def first_analysis(q, g, parts, chunks):
    n, _, height, ny = parts[0].shape
    members = n * sum(part.shape[1] for part in parts)
    if HALO > height:
        chunks = 0
    sends = [(HALO, members // chunks, ny)] * (2 * chunks) if chunks else []
    return pl.pallas_call(
        functools.partial(first_analysis_kernel, g.shape[1], len(parts), chunks),
        grid=(height // SUB,),
        in_specs=[
            pl.BlockSpec(memory_space=pltpu.SMEM),
            pl.BlockSpec(g.shape, lambda i: (0, 0, 0, 0)),
        ]
        + [pl.BlockSpec((n, part.shape[1], SUB, ny), lambda i: (0, 0, i, 0)) for part in parts],
        out_specs=[pl.BlockSpec((SUB, members, ny), lambda i: (i, 0, 0))]
        + [pl.BlockSpec(s, lambda i: (0, 0, 0)) for s in sends],
        out_shape=[jax.ShapeDtypeStruct((height, members, ny), F32)]
        + [jax.ShapeDtypeStruct(s, F32) for s in sends],
        name="first_analysis",
    )(q, g, *parts)


def last_analysis_kernel(nparts, at_ref, g_ref, *refs):
    xs, out_ref = refs[:nparts], refs[nparts]
    count = g_ref.shape[1]
    n, _, mine, rows, ny = out_ref.shape
    for p in range(rows // PR):
        g = g_ref[0, p]
        x = jnp.concatenate(
            [jnp.concatenate([part[PR * p + i] for part in xs], axis=0) for i in range(PR)], axis=1
        )
        y = mix(g, x)
        for i in range(PR):
            for j in range(mine):
                out_ref[:, 0, j, PR * p + i, :] = y[j * n : (j + 1) * n, i * ny : (i + 1) * ny]


def last_analysis(at, g, xs, n):
    quarters, count, members, _ = g.shape
    ny = xs[0].shape[2]
    rows = count * PR
    mine = members // n
    return pl.pallas_call(
        functools.partial(last_analysis_kernel, len(xs)),
        grid_spec=pltpu.PrefetchScalarGridSpec(
            num_scalar_prefetch=1,
            grid=(quarters,),
            in_specs=[pl.BlockSpec((1, count, members, members), lambda i, at: (i, 0, 0, 0))]
            + [pl.BlockSpec((rows, part.shape[1], ny), lambda i, at: (at[i], 0, 0)) for part in xs],
            out_specs=pl.BlockSpec((n, 1, mine, rows, ny), lambda i, at: (0, i, 0, 0, 0)),
        ),
        out_shape=jax.ShapeDtypeStruct((n, quarters, mine, rows, ny), F32),
        name="last_analysis",
    )(at, g, *xs)


def assemble_kernel(nv, a_ref, b_ref, out_ref):
    mine, _, height, ny = out_ref.shape
    rows = height // nv
    for v in range(nv):
        for c in range(nv):
            src = a_ref[v, 0] if c == 0 else b_ref[v, c - 1]
            at = (v ^ c) * rows
            whole = interleave(src.reshape(mine * rows, ny)).reshape(mine, rows, ny) if rows % SUB == 0 else None
            for j in range(mine):
                out_ref[j, v, at : at + rows, :] = interleave(src[j]) if whole is None else whole[j]


def assemble(nv, a, b, nx):
    n, _, mine, rows, ny = a.shape
    groups = n // nv
    height = nx // groups
    spot = lambda g: lax.select(g % 2 == 0, g // 2, groups - 1 - g // 2) if groups > 1 else g
    return pl.pallas_call(
        functools.partial(assemble_kernel, nv),
        grid=(groups,),
        in_specs=[
            pl.BlockSpec((nv, 1, mine, rows, ny), lambda g: (g, 0, 0, 0, 0)),
            pl.BlockSpec((nv, nv - 1, mine, rows, ny), lambda g: (g, 0, 0, 0, 0)),
        ],
        out_specs=pl.BlockSpec((mine, nv, height, ny), lambda g: (0, 0, spot(g), 0)),
        out_shape=jax.ShapeDtypeStruct((mine, nv, nx, ny), F32),
        name="assemble",
    )(a, b)


def local(n, ensemble, flow_speed, spreading, obs_values, obs_var, obs_block, readers, counts):
    mine, nv, nx, ny = ensemble.shape
    members = mine * n
    nobs = obs_var.shape[0]
    patches, slots = readers.shape
    groups = n // nv
    height = nx // groups
    count = patches // n
    width = nobs // n
    nbr, nbc = nx // BLOCK, ny // BLOCK
    per_row = nobs // nbr
    half = ny // 2

    place = [2 * r if 2 * r < groups else 2 * (groups - 1 - r) + 1 for r in range(groups)]
    owner_rows = [place.index(g) for g in range(groups)]
    device = lambda s: nv * place[(s // nv) % groups] + s % nv

    me = lax.axis_index("dev")
    q = lax.rem(me, nv)
    g = me // nv
    r = jnp.where(g % 2 == 0, g // 2, groups - 1 - g // 2) if groups > 1 else g * 0
    spot = r * nv + q
    q_ref = q.reshape(1).astype(jnp.int32)

    def send(x, hop):
        return lax.ppermute(x, "dev", [(device(s), device((s + hop) % n)) for s in range(n)])

    def swap(x, c):
        return lax.ppermute(x, "dev", [(d, d ^ c) for d in range(n)])

    obs_col = (obs_block % nbc).reshape(nbr, per_row)
    obs_v = (obs_block // (nbr * nbc)).reshape(nbr, per_row)
    lanes = max(128, nbc)

    def table(a):
        a = a.reshape(SUB, nbr // SUB, per_row).transpose(1, 0, 2).reshape(nbr, per_row)
        return jnp.pad(a, ((0, 0), (0, lanes - per_row)))

    col_table, var_table = table(obs_col), table(obs_v)

    forecast = lambda first, many: member_forecast(
        first, many, ensemble, flow_speed, spreading, col_table, var_table, owner_rows
    )
    send_all = lambda x: lax.all_to_all(x, "dev", 0, 0, tiled=True)
    cuts = [(0, 1), (1, mine - 1)] if mine > 1 else [(0, 1)]
    parts, observed = [], []
    for first, many in cuts:
        fields, hx = forecast(first, many)
        parts.append(fields.reshape(n, many, height, ny))
        observed.append(hx)
    arrived = [send_all(parts[0])]
    observed = jnp.concatenate(observed, 0)[:, :, :per_row]
    observed = observed.reshape(mine, nbr // SUB, SUB, per_row).transpose(0, 2, 1, 3).reshape(mine, groups, nv, width)
    observed = jnp.stack([observed[:, r0] for r0 in owner_rows], 0).transpose(0, 2, 1, 3).reshape(n, mine, width)
    observed = send_all(observed)
    if mine > 1:
        rest, observed = lax.optimization_barrier((parts[1], observed))
        arrived.append(send_all(rest))
    hx = observed.transpose(1, 0, 2).reshape(members, width)

    first = spot * count
    chosen = lax.dynamic_slice_in_dim(readers, first, count, 0)
    my_counts = lax.dynamic_slice_in_dim(counts, first, count, 0)
    patch_index = first + jnp.arange(count, dtype=jnp.int32)
    obs_row = (chosen * nbr // nobs).astype(F32) * BLOCK + 0.5 * (BLOCK - 1)
    patch_row = patch_index.astype(F32) * PR + 0.5 * (PR - 1)
    gap = jnp.abs(obs_row - patch_row[:, None])
    distance = jnp.minimum(gap, nx - gap)
    taper = jnp.exp(-0.5 * (distance / TAPER_ROWS) ** 2)
    listed = jnp.arange(slots, dtype=jnp.int32) < my_counts[:, None]
    weight = jnp.where(listed, taper / obs_var[chosen], 0.0)[:, None, :]
    values = obs_values[:, chosen][:, :, None, :]
    chosen = chosen[:, None, :]

    reach = -(-NEAR * per_row // width) + (1 if width < per_row else 0)
    reach = min(reach, (n - 1) // 2)
    owner = jnp.arange(patches, dtype=jnp.int32)[:, None] // count
    away = lax.rem(readers // width - owner + (n + reach), n)
    read = jnp.arange(slots, dtype=jnp.int32) < counts[:, None]
    near = jnp.all((away <= 2 * reach) | ~read)

    start = r * height - HALO + nx
    take = lambda a: lax.dynamic_slice_in_dim(jnp.concatenate([a, a, a], -2), start, height + 2 * HALO, a.ndim - 2)
    my_spread = take(lax.dynamic_index_in_dim(spreading, q, 0, keepdims=True))
    raw = jnp.concatenate([my_spread, 0.5 * take(flow_speed)], 0)
    raw = raw.reshape(raw.shape[:2] + (half, 2)).transpose(0, 1, 3, 2).reshape(raw.shape)
    raw = jnp.broadcast_to(raw[:, :, None, :], raw.shape[:2] + (SUB, ny))
    block_rows = height // BLOCK
    group_col = lax.dynamic_slice_in_dim(obs_col, r * block_rows, block_rows, 0)
    group_var = lax.dynamic_slice_in_dim(obs_v, r * block_rows, block_rows, 0)
    column = (jnp.arange(ny, dtype=jnp.int32) % half) // (BLOCK // 2)
    pick = jnp.where(
        (column[None, :, None] == group_col[:, None, :]) & (group_var[:, None, :] == q),
        1.0 / (BLOCK * BLOCK),
        0.0,
    ).astype(BF16)

    def solve(cycle, hx):
        shifts = list(range(-reach, reach + 1))
        blocks = [hx if o == 0 else send(hx, -o) for o in shifts]
        base = (spot + jnp.array(shifts, jnp.int32) + n) % n * width

        def close(hx, *blocks):
            return select(base, chosen, [b[None] for b in blocks])

        def far(hx, *blocks):
            every = lax.all_to_all(jnp.broadcast_to(hx[None], (n,) + hx.shape), "dev", 0, 0, tiled=True)
            owner = [(owner_rows[d // nv] * nv + d % nv) * width for d in range(n)]
            return select(jnp.array(owner, jnp.int32), chosen, [every])

        picked = lax.cond(near, close, far, hx, *blocks)
        return transforms(picked, weight, values[cycle])

    own = solve(0, hx)
    every = jnp.stack([own] + [swap(own, c) for c in range(1, nv)])
    every, raw, pick, values = lax.optimization_barrier((every, raw, pick, values))
    chunks = 2 if HALO <= height else 1
    state, *sends = first_analysis(q_ref, every, arrived, chunks)

    if not sends:
        sends = [state, state]
    advanced, partial = [], []
    for c in range(chunks):
        lo, hi = [], []
        left, hop = HALO, 1
        while left > 0:
            rows_k = min(left, height)
            down, up = sends[2 * c], sends[2 * c + 1]
            lo.insert(0, send(down[down.shape[0] - rows_k :], hop * nv))
            hi.append(send(up[:rows_k], -hop * nv))
            left -= rows_k
            hop += 1
        lo = lo[0] if len(lo) == 1 else jnp.concatenate(lo, 0)
        hi = hi[0] if len(hi) == 1 else jnp.concatenate(hi, 0)
        out, hx = group_forecast(c, min(64, lo.shape[1]), state, lo, hi, raw, pick)
        advanced.append(out)
        partial.append(hx)
    partial = (jnp.concatenate(partial, 0) if chunks > 1 else partial[0]).reshape(members, nv, width)
    pieces = [lax.dynamic_index_in_dim(partial, q, 1, keepdims=False)]
    for c in range(1, nv):
        other = lax.dynamic_index_in_dim(partial, lax.bitwise_xor(q, c), 1, keepdims=False)
        pieces.append(swap(other, c))
    hx = functools.reduce(lambda a, b: a + b, pieces)

    own = solve(1, hx)
    others = [swap(own, c) for c in range(1, nv)]
    front = last_analysis(q_ref, own[None], advanced, n)
    at = lax.bitwise_xor(q, jnp.arange(1, nv, dtype=jnp.int32))
    back = last_analysis(at, jnp.stack(others), advanced, n)
    return assemble(nv, send_all(front), send_all(back), nx)


def solution(mesh):
    n = mesh.shape["dev"]
    return jax.shard_map(
        functools.partial(local, n),
        mesh=mesh,
        in_specs=(P("dev", None, None, None), P(), P(), P(), P(), P(), P(), P()),
        out_specs=P("dev", None, None, None),
        check_vma=False,
    )
```
